256 devices in a mesh: gx: 32 (over z, y_hi, core), gy: 8 (over x, y_lo).
Axes of the slice: x: 4, y: 4 (y_hi: 2, y_lo: 2; y = y_hi * 2 + y_lo), z: 8, core: 2. Of those that a mesh axis runs over, the one named last changes fastest.
Arguments:
- hamiltonian: bfloat16 [64, 16, 8, 128, 128], P('gx', 'gy'), may hold values from -0.078125 to 0.078125
- neighbours: int32 [64, 16, 8], P('gx', 'gy'), may hold values from 0 to 8, as said below
- probe_seeds: int32 [256], replicated, may hold values from 0 to 1073741823
- coefficients: float32 [5], replicated, may hold values from 0.3 to 1
- cotangent: bfloat16 [64, 16, 128, 256], P('gx', 'gy'), may hold values from -6 to 6
Outputs:
- density: float32 [64, 16, 128, 256], P('gx', 'gy')
- grad_hamiltonian: bfloat16 [64, 16, 8, 128, 128], P('gx', 'gy')
The draws below stay inside these ranges and needn't reach their ends.
Inputs may be any that keep to these rules, and one draw needn't show every extreme that they name: `neighbours`: each block's list holds 8 different codes.
All inputs are finite; a program needn't handle non-finite values.
Results may differ from the reference program's by a relative error of at most 0.0064.
Values may be sent and summed in bfloat16 or wider, within the bound.
A program may use at most 64 MiB of HBM per device.

```python
import jax
import jax.numpy as jnp

B = 128
P_SIZE = 256
K = 8
TERMS = 5
GBX = 64
GBY = 16


def draw_neighbours(key, part):
    missing = jax.random.randint(key, (GBX, GBY, 1), 0, 9, dtype=jnp.int32)
    slot_index = jnp.arange(K, dtype=jnp.int32)
    return slot_index + (slot_index >= missing).astype(jnp.int32)


def place_ends(entries, own_key, least, top_value):
    dims = entries.shape
    place = [jax.random.randint(jax.random.fold_in(own_key, axis), (), 0, dims[axis]) for axis in range(len(dims))]
    entries = entries.at[tuple(place)].set(least)
    longest = dims.index(max(dims))
    place[longest] = (place[longest] + 1) % dims[longest]
    return entries.at[tuple(place)].set(top_value)


def block_levels(rng, shape, split, smallest, top_value):
    def one(dim, blocks):
        draws = jax.random.uniform(jax.random.fold_in(jax.random.fold_in(rng, 6), dim), (blocks,), jnp.float32, smallest / len(split), top_value / len(split))
        return jnp.repeat(jnp.exp(draws), shape[dim] // blocks).reshape((-1,) + (1,) * (len(shape) - dim - 1))

    level = one(*split[0])
    for cut in split[1:]:
        level = level * one(*cut)
    return level


def gaussian(rng, dims, spread, most, pieces=(), kind=jnp.bfloat16):
    gain = block_levels(rng, dims, pieces, -0.22, 0.18) if pieces else 1.0
    drawn = jax.random.normal(rng, dims, jnp.float32) * spread * gain
    return jnp.minimum(jnp.maximum(drawn, -most), most).astype(kind)


def setup_inputs(seed: int = 0) -> dict:
    key_of = jax.random.split(jax.random.key(seed), 6)
    return {
        "hamiltonian": gaussian(key_of[0], (GBX, GBY, K, B, B), (25 * K * B // 4) ** -0.5, 0.078125, ((0, 32), (1, 8))),
        "neighbours": draw_neighbours(jax.random.fold_in(key_of[5], 71), 0),
        "probe_seeds": place_ends(jax.random.randint(key_of[2], (P_SIZE,), 0, 1073741824), jax.random.fold_in(key_of[2], 1), 0, 1073741823).astype(jnp.int32),
        "coefficients": jnp.clip(jax.random.uniform(key_of[3], (TERMS,), jnp.float32, 0.3, 1.0), 0.3, 1.0),
        "cotangent": gaussian(key_of[4], (GBX, GBY, B, P_SIZE), 1.0, 6.0, ((0, 32), (1, 8))),
    }


offset_table = tuple((offset_code // 3 - 1, offset_code % 3 - 1) for offset_code in range(9))


def probe_signs(global_rows, seed_values):
    hashed = global_rows[..., None] * jnp.int32(-1640531535)
    hashed = hashed ^ seed_values
    hashed = hashed ^ (hashed >> 15)
    hashed = hashed * jnp.int32(739982445)
    hashed = hashed ^ (hashed >> 12)
    parity = (hashed >> 7) & 1
    return (1 - 2 * parity).astype(jnp.float32)


def select_blocks(hamiltonian, neighbours, offset_code):
    chosen = jnp.zeros(hamiltonian.shape[:2] + hamiltonian.shape[3:], jnp.float32)
    for column in range(hamiltonian.shape[2]):
        chosen = chosen + jnp.where((neighbours[:, :, column] == offset_code)[:, :, None, None],
                                    hamiltonian[:, :, column].astype(jnp.float32), 0.0)
    return chosen.astype(jnp.bfloat16)


def forward_apply(selected, field_bf16):
    summed = jnp.zeros(field_bf16.shape, jnp.float32)
    for offset_code, (step_x, step_y) in enumerate(offset_table):
        moved = jnp.roll(field_bf16, (-step_x, -step_y), (0, 1)).astype(jnp.float32)
        summed = summed + jnp.einsum('abxy,abyp->abxp', selected[offset_code].astype(jnp.float32), moved)
    return summed


def transpose_apply(selected, field_bf16):
    summed = jnp.zeros(field_bf16.shape, jnp.float32)
    for offset_code, (step_x, step_y) in enumerate(offset_table):
        product = jnp.einsum('abyx,abyp->abxp', selected[offset_code].astype(jnp.float32), field_bf16.astype(jnp.float32))
        summed = summed + jnp.roll(product, (step_x, step_y), (0, 1))
    return summed


def reference(hamiltonian, neighbours, probe_seeds, coefficients, cotangent):
    place_x = jnp.arange(GBX, dtype=jnp.int32)
    place_y = jnp.arange(GBY, dtype=jnp.int32)
    orbital = jnp.arange(B, dtype=jnp.int32)
    global_rows = (place_x[:, None] * GBY + place_y[None, :])[:, :, None] * B + orbital[None, None, :]
    start_term = probe_signs(global_rows, probe_seeds)
    selected = [select_blocks(hamiltonian, neighbours, offset_code) for offset_code in range(9)]
    rounded_terms = [start_term.astype(jnp.bfloat16)]
    previous = start_term
    current = forward_apply(selected, rounded_terms[0])
    density = coefficients[0] * start_term + coefficients[1] * current
    for index in range(2, TERMS):
        rounded_terms.append(current.astype(jnp.bfloat16))
        following = 2.0 * forward_apply(selected, rounded_terms[-1]) - previous
        previous, current = current, following
        density = density + coefficients[index] * current
    seed_field = cotangent.astype(jnp.float32)
    adjoints = {}
    adjoint_rounded = {}
    for index in range(TERMS - 1, 0, -1):
        value = coefficients[index] * seed_field
        if index + 1 < TERMS:
            value = value + 2.0 * transpose_apply(selected, adjoint_rounded[index + 1])
        if index + 2 < TERMS:
            value = value - adjoints[index + 2]
        adjoints[index] = value
        adjoint_rounded[index] = value.astype(jnp.bfloat16)
    gradient = jnp.zeros(hamiltonian.shape, jnp.float32)
    for offset_code, (step_x, step_y) in enumerate(offset_table):
        block_grad = jnp.zeros((GBX, GBY, B, B), jnp.float32)
        for index in range(1, TERMS):
            factor = 1.0 if index == 1 else 2.0
            moved = jnp.roll(rounded_terms[index - 1], (-step_x, -step_y), (0, 1)).astype(jnp.float32)
            weighted = (adjoint_rounded[index] * factor).astype(jnp.float32)
            block_grad = block_grad + jnp.einsum('abxp,abyp->abxy', weighted, moved)
        gradient = gradient + jnp.where((neighbours == offset_code)[..., None, None], block_grad[:, :, None], 0.0)
    return density, (gradient * (1.0 / P_SIZE)).astype(jnp.bfloat16)
```

```python
import functools

import jax
import jax.numpy as jnp
from jax import lax
from jax.experimental import pallas as pl
from jax.experimental.pallas import tpu as pltpu
from jax.sharding import PartitionSpec as P

MESH = pl.DeviceIdType.MESH
BF16 = jnp.bfloat16
F32 = jnp.float32
B = 128


def mm(left, right):
    return jnp.dot(left, right, preferred_element_type=F32)


def mm_nt(left, right):
    return lax.dot_general(left, right, (((1,), (1,)), ((), ())), preferred_element_type=F32)


def kernel(
    nx, ny, nb,
    h_ref, nbr_ref, seed_ref, coef_ref, cot_ref,
    den_ref, grad_ref,
    hf, ht, tp, tf, av, af, acc, qf, gacc,
    s0, s3, rd, rp, sc, rg,
    fsend, frecv, asend, arecv,
):
    gx = lax.axis_index("gx")
    gy = lax.axis_index("gy")
    odd = lax.rem(gx, 2)
    out_x = lax.rem(gx + nx - 1 + 2 * odd, nx)
    par_x = gx + 1 - 2 * odd
    right_y = lax.rem(gy + 1, ny)
    left_y = lax.rem(gy + ny - 1, ny)
    partner = (par_x, gy)
    right = (gx, right_y)
    left = (gx, left_y)
    diag_r = (out_x, right_y)
    diag_l = (out_x, left_y)

    barrier = pltpu.get_barrier_semaphore()
    for who in (partner, right, left, diag_r, diag_l):
        pl.semaphore_signal(barrier, inc=1, device_id=who, device_id_type=MESH)

    def real_row(a):
        return a + odd * (1 - 2 * a)

    zero = jnp.zeros((B, B), BF16)
    for a in range(2):
        ra = real_row(a)
        for d in range(3):
            hf[a, d, 0:B, 3 * B : 4 * B] = zero
            hf[a, d, B : 2 * B, 0:B] = zero
            ht[a, d, 3 * B : 4 * B, 0:B] = zero
            ht[a, d, 0:B, B : 2 * B] = zero
        for b in range(2):
            listed = [nbr_ref[(ra * 2 + b) * 8 + k] for k in range(8)]
            for d in range(3):
                rdx = d + odd * (2 - 2 * d)
                for dy in range(3):
                    code = rdx * 3 + dy
                    place = jnp.int32(0)
                    for k in range(8):
                        place = jnp.where(listed[k] == code, k + 1, place)
                    found = jnp.where(place > 0, 1.0, 0.0)
                    block = h_ref[ra, b, jnp.maximum(place - 1, 0)].astype(F32) * found
                    j = b + dy
                    hf[a, d, b * B : (b + 1) * B, j * B : (j + 1) * B] = block.astype(BF16)
                    ht[a, d, j * B : (j + 1) * B, b * B : (b + 1) * B] = block.T.astype(BF16)

    def coef(t):
        return coef_ref[t]

    def cot_row(a):
        return cot_ref[real_row(a)].reshape(2 * B, cot_ref.shape[3]).astype(F32)

    def copy(src, dst, sems, where, who):
        return pltpu.make_async_remote_copy(
            src_ref=src, dst_ref=dst, send_sem=sems[0].at[where], recv_sem=sems[1].at[where],
            device_id=who, device_id_type=MESH,
        )

    def blk(ref, c, n=1):
        return ref.at[c * B : (c + n) * B]

    fs = (fsend, frecv)
    fcopies = {}
    for t in (1, 2, 3):
        r = t - 1
        t0, t1, t2, t3 = (tp.at[t, i] for i in range(4))
        fcopies[t] = dict(
            r1=copy(blk(t1, 2), blk(t1, 0), fs, (r, 0), right),
            l1=copy(blk(t1, 1), blk(t1, 3), fs, (r, 1), left),
            r2=copy(blk(t2, 2), blk(t2, 0), fs, (r, 2), right),
            l2=copy(blk(t2, 1), blk(t2, 3), fs, (r, 3), left),
            dra=copy(blk(t1, 2), blk(t0, 0), fs, (r, 4), diag_r),
            dla=copy(blk(t1, 1), blk(t0, 3), fs, (r, 5), diag_l),
            drb=copy(blk(t1, 3), blk(t0, 1), fs, (r, 6), diag_r),
            dlb=copy(blk(t1, 0), blk(t0, 2), fs, (r, 7), diag_l),
            pa=copy(blk(t2, 1, 2), blk(t3, 1, 2), fs, (r, 8), partner),
            p0=copy(blk(t2, 0), blk(t3, 0), fs, (r, 9), partner),
            p3=copy(blk(t2, 3), blk(t3, 3), fs, (r, 10), partner),
        )
    as_ = (asend, arecv)
    acopies = {}
    for r in range(3):
        acopies[r] = dict(
            dl=copy(blk(s0.at[r], 0, 2), blk(rd.at[r], 2, 2), as_, (r, 0), diag_l),
            dr=copy(blk(s0.at[r], 2, 2), blk(rd.at[r], 0, 2), as_, (r, 1), diag_r),
            p=copy(s3.at[r], rp.at[r], as_, (r, 2), partner),
            l1=copy(sc.at[r, 0, 0], rg.at[r, 0, 1], as_, (r, 3), left),
            r1=copy(sc.at[r, 0, 1], rg.at[r, 0, 0], as_, (r, 4), right),
            l2=copy(sc.at[r, 1, 0], rg.at[r, 1, 1], as_, (r, 5), left),
            r2=copy(sc.at[r, 1, 1], rg.at[r, 1, 0], as_, (r, 6), right),
        )

    def adj_outer(r):
        t = 4 - r
        s0[r] = mm(ht[0, 0], av[t, 0]).astype(BF16)
        acopies[r]["dl"].start()
        acopies[r]["dr"].start()
        s3[r] = mm(ht[1, 2], av[t, 1]).astype(BF16)
        acopies[r]["p"].start()

    def adj_inner(r):
        t = 4 - r
        qf[0] = mm(ht[0, 1], av[t, 0]) + mm(ht[1, 0], av[t, 1])
        qf[1] = mm(ht[0, 2], av[t, 0]) + mm(ht[1, 1], av[t, 1])

    def adj_side(r):
        c = acopies[r]
        c["p"].wait_recv()
        sc[r, 1, 0] = (qf[1, 0:B] + rp[r, 0:B].astype(F32)).astype(BF16)
        c["l2"].start()
        sc[r, 1, 1] = (qf[1, 3 * B : 4 * B] + rp[r, 3 * B : 4 * B].astype(F32)).astype(BF16)
        c["r2"].start()
        c["dl"].wait_recv()
        c["dr"].wait_recv()
        sc[r, 0, 0] = (qf[0, 0:B] + rd[r, 0:B].astype(F32)).astype(BF16)
        c["l1"].start()
        sc[r, 0, 1] = (qf[0, 3 * B : 4 * B] + rd[r, 3 * B : 4 * B].astype(F32)).astype(BF16)
        c["r1"].start()

    def adj_finish(r):
        t = 3 - r
        c = acopies[r]
        for name in ("l2", "r2", "l1", "r1"):
            c[name].wait_recv()
        for a in range(2):
            got = rd if a == 0 else rp
            for b in range(2):
                rows = slice((1 + b) * B, (2 + b) * B)
                own = slice(b * B, (b + 1) * B)
                total = qf[a, rows] + got[r, rows].astype(F32) + rg[r, a, b].astype(F32)
                value = coef(t) * cot_ref[real_row(a), b].astype(F32) + 2.0 * total
                if t == 2:
                    value = value - coef(4) * cot_ref[real_row(a), b].astype(F32)
                if t == 1:
                    value = value - af[a, own]
                if t == 3:
                    af[a, own] = value
                av[t, a, own] = value.astype(BF16)

    def apply_row(t, a):
        return mm(hf[a, 0], tp[t, a]) + mm(hf[a, 1], tp[t, a + 1]) + mm(hf[a, 2], tp[t, a + 2])

    def own(t, a):
        return tp[t, a + 1, B : 3 * B]

    def term_row(t, a):
        value = apply_row(t - 1, a)
        if t == 1:
            acc[a] = coef(0) * own(0, a).astype(F32) + coef(1) * value
        else:
            before = own(0, a).astype(F32) if t == 2 else tf[t - 3, a]
            value = 2.0 * value - before
            acc[a] = acc[a] + coef(t) * value
        if t < 3:
            tf[t - 1, a] = value
        if t < 4:
            tp[t, a + 1, B : 3 * B] = value.astype(BF16)

    def term(t):
        c = fcopies[t]
        term_row(t, 0)
        for name in ("r1", "l1", "dra", "dla"):
            c[name].start()
        term_row(t, 1)
        for name in ("r2", "l2", "pa"):
            c[name].start()

    def relay(t):
        c = fcopies[t]
        c["r1"].wait_recv()
        c["dlb"].start()
        c["l1"].wait_recv()
        c["drb"].start()
        c["r2"].wait_recv()
        c["p0"].start()
        c["l2"].wait_recv()
        c["p3"].start()

    def halo(t):
        c = fcopies[t]
        for name in ("pa", "p0", "p3", "dra", "dla", "drb", "dlb"):
            c[name].wait_recv()

    def gradient(t, first=False):
        for a in range(2):
            for d in range(3):
                full = mm_nt(av[t, a], tp[t - 1, a + d])
                for b in range(2):
                    for dy in range(3):
                        j = b + dy
                        piece = full[b * B : (b + 1) * B, j * B : (j + 1) * B]
                        if not first:
                            piece = piece + gacc[a, b, d * 3 + dy]
                        gacc[a, b, d * 3 + dy] = piece

    for a in range(2):
        av[4, a] = (coef(4) * cot_row(a)).astype(BF16)
    pl.semaphore_wait(barrier, 5)
    adj_outer(0)

    width = tp.shape[3]
    lane_rows = lax.broadcasted_iota(jnp.int32, (B, width), 0) * jnp.int32(-1640531535)
    seeds = jnp.broadcast_to(seed_ref[...], (B, width))
    for i in range(4):
        ri = i + odd * (3 - 2 * i)
        px = lax.rem(gx * 2 + ri - 1 + 2 * nx, 2 * nx)
        for j in range(4):
            py = lax.rem(gy * 2 + j - 1 + 2 * ny, 2 * ny)
            base = ((px * (2 * ny) + py) * B) * jnp.int32(-1640531535)
            hashed = (lane_rows + base) ^ seeds
            hashed = hashed ^ (hashed >> 15)
            hashed = hashed * jnp.int32(739982445)
            hashed = hashed ^ (hashed >> 12)
            tp[0, i, j * B : (j + 1) * B] = jnp.where((hashed & 128) == 0, 1.0, -1.0).astype(BF16)

    term(1)
    adj_inner(0)
    adj_side(0)
    relay(1)
    adj_finish(0)
    adj_outer(1)
    halo(1)
    term(2)
    adj_inner(1)
    adj_side(1)
    relay(2)
    adj_finish(1)
    adj_outer(2)
    halo(2)
    term(3)
    adj_inner(2)
    adj_side(2)
    relay(3)
    gradient(2, first=True)
    gradient(3)
    adj_finish(2)
    halo(3)
    term_row(4, 0)
    term_row(4, 1)
    for a in range(2):
        ra = real_row(a)
        for b in range(2):
            den_ref[ra, b] = acc[a, b * B : (b + 1) * B]
    gradient(4)
    for a in range(2):
        for d in range(3):
            full = mm_nt(av[1, a], tp[0, a + d])
            for b in range(2):
                for dy in range(3):
                    j = b + dy
                    piece = full[b * B : (b + 1) * B, j * B : (j + 1) * B]
                    gacc[a, b, d * 3 + dy] = (piece + 2.0 * gacc[a, b, d * 3 + dy]) * (1.0 / width)
    for a in range(2):
        ra = real_row(a)
        for b in range(2):
            for k in range(8):
                code = nbr_ref[(ra * 2 + b) * 8 + k]
                rdx = code // 3
                mine = rdx + odd * (2 - 2 * rdx)
                grad_ref[ra, b, k] = gacc[a, b, mine * 3 + code - 3 * rdx].astype(BF16)

    for group in list(fcopies.values()) + list(acopies.values()):
        for one in group.values():
            one.wait_send()


def shards(nx, ny, hamiltonian, neighbours, probe_seeds, coefficients, cotangent):
    width = cotangent.shape[3]
    whole = pl.BlockSpec(memory_space=pltpu.VMEM)
    scalars = pl.BlockSpec(memory_space=pltpu.SMEM)
    vmem = pltpu.VMEM
    nb = 2
    return pl.pallas_call(
        functools.partial(kernel, nx, ny, nb),
        out_shape=(
            jax.ShapeDtypeStruct(cotangent.shape, F32),
            jax.ShapeDtypeStruct(hamiltonian.shape, BF16),
        ),
        in_specs=[whole, scalars, whole, scalars, whole],
        out_specs=(whole, whole),
        scratch_shapes=[
            vmem((2, 3, 2 * B, 4 * B), BF16),
            vmem((2, 3, 4 * B, 2 * B), BF16),
            vmem((4, 4, 4 * B, width), BF16),
            vmem((2, 2, 2 * B, width), F32),
            vmem((5, 2, 2 * B, width), BF16),
            vmem((2, 2 * B, width), F32),
            vmem((2, 2 * B, width), F32),
            vmem((2, 4 * B, width), F32),
            vmem((2, 2, 9, B, B), F32),
            vmem((3, 4 * B, width), BF16),
            vmem((3, 4 * B, width), BF16),
            vmem((3, 4 * B, width), BF16),
            vmem((3, 4 * B, width), BF16),
            vmem((3, 2, 2, B, width), BF16),
            vmem((3, 2, 2, B, width), BF16),
            pltpu.SemaphoreType.DMA((3, 11)),
            pltpu.SemaphoreType.DMA((3, 11)),
            pltpu.SemaphoreType.DMA((3, 7)),
            pltpu.SemaphoreType.DMA((3, 7)),
        ],
        compiler_params=pltpu.CompilerParams(collective_id=0, has_side_effects=True),
    )(hamiltonian, neighbours.reshape(-1), probe_seeds.reshape(1, -1), coefficients, cotangent)


def solution(mesh):
    placed = (
        P("gx", "gy", None, None, None),
        P("gx", "gy", None),
        P(),
        P(),
        P("gx", "gy", None, None),
    )
    return jax.shard_map(
        functools.partial(shards, mesh.shape["gx"], mesh.shape["gy"]),
        mesh=mesh,
        in_specs=placed,
        out_specs=(P("gx", "gy", None, None), P("gx", "gy", None, None, None)),
        check_vma=False,
    )
```

```python
import functools

import jax
import jax.numpy as jnp
from jax import lax
from jax.experimental import pallas as pl
from jax.experimental.pallas import tpu as pltpu
from jax.sharding import PartitionSpec as P

MESH = pl.DeviceIdType.MESH
BF16 = jnp.bfloat16
F32 = jnp.float32
B = 128
HALVES = 2


def mm(left, right):
    return jnp.dot(left, right, preferred_element_type=F32)


def mm_nt(left, right):
    return lax.dot_general(left, right, (((1,), (1,)), ((), ())), preferred_element_type=F32)


def joined(ref, *where):
    return jnp.concatenate([ref[(h,) + where] for h in range(HALVES)], axis=1)


class Copy:
    def __init__(self, *args):
        self.args = args
        self.arrived = False

    def make(self):
        src, dst, sems, where, who = self.args
        return pltpu.make_async_remote_copy(
            src_ref=src, dst_ref=dst, send_sem=sems[0].at[where], recv_sem=sems[1].at[where],
            device_id=who, device_id_type=MESH,
        )

    def start(self):
        self.make().start()

    def recv(self):
        if not self.arrived:
            self.arrived = True
            self.make().wait_recv()

    def sent(self):
        self.make().wait_send()


def kernel(
    nx, ny,
    h_hbm, nbr_ref, seed_ref, coef_ref, cot_hbm,
    tp, av, gacc, den_ref,
    h_outer, h_inner, cot_ref,
    hf, ht, tf, af, acc, qf,
    s0, s3, rd, rp, sc, rg,
    fsend, frecv, asend, arecv, isem,
):
    gx = lax.axis_index("gx")
    gy = lax.axis_index("gy")
    odd = lax.rem(gx, 2)
    out_x = lax.rem(gx + nx - 1 + 2 * odd, nx)
    par_x = gx + 1 - 2 * odd
    right_y = lax.rem(gy + 1, ny)
    left_y = lax.rem(gy + ny - 1, ny)
    partner = (par_x, gy)
    right = (gx, right_y)
    left = (gx, left_y)
    diag_r = (out_x, right_y)
    diag_l = (out_x, left_y)

    barrier = pltpu.get_barrier_semaphore()
    for who in (partner, right, left, diag_r, diag_l):
        pl.semaphore_signal(barrier, inc=1, device_id=who, device_id_type=MESH)
    def real_row(a):
        return a + odd * (1 - 2 * a)

    in_cot = pltpu.make_async_copy(cot_hbm, cot_ref, isem.at[0])
    in_h = [
        pltpu.make_async_copy(h_hbm.at[real_row(a)], ref, isem.at[1 + a])
        for a, ref in enumerate((h_outer, h_inner))
    ]
    in_cot.start()
    in_h[0].start()
    in_h[1].start()

    width = tp.shape[4]

    def coef(t):
        return coef_ref[t]

    def signs(rows):
        whole = HALVES * width
        lane_rows = lax.broadcasted_iota(jnp.int32, (B, whole), 0) * jnp.int32(-1640531535)
        seeds = jnp.broadcast_to(seed_ref[...], (B, whole))
        for i in rows:
            ri = i + odd * (3 - 2 * i)
            px = lax.rem(gx * 2 + ri - 1 + 2 * nx, 2 * nx)
            for j in range(4):
                py = lax.rem(gy * 2 + j - 1 + 2 * ny, 2 * ny)
                base = ((px * (2 * ny) + py) * B) * jnp.int32(-1640531535)
                hashed = (lane_rows + base) ^ seeds
                hashed = hashed ^ (hashed >> 15)
                hashed = hashed * jnp.int32(739982445)
                hashed = hashed ^ (hashed >> 12)
                sign = jnp.where((hashed & 128) == 0, 1.0, -1.0).astype(BF16)
                for h in range(HALVES):
                    tp[h, 0, i, j * B : (j + 1) * B] = sign[:, h * width : (h + 1) * width]

    def select(a, d):
        zero = jnp.zeros((B, B), BF16)
        ra = real_row(a)
        rdx = d + odd * (2 - 2 * d)
        hf[a, d, 0:B, 3 * B : 4 * B] = zero
        hf[a, d, B : 2 * B, 0:B] = zero
        ht[a, d, 3 * B : 4 * B, 0:B] = zero
        ht[a, d, 0:B, B : 2 * B] = zero
        for b in range(2):
            for dy in range(3):
                code = rdx * 3 + dy
                place = jnp.int32(0)
                for k in range(8):
                    place = jnp.where(nbr_ref[ra, b, k] == code, k + 1, place)
                found = jnp.where(place > 0, 1.0, 0.0)
                block = (h_outer, h_inner)[a][b, jnp.maximum(place - 1, 0)].astype(F32) * found
                j = b + dy
                hf[a, d, b * B : (b + 1) * B, j * B : (j + 1) * B] = block.astype(BF16)
                ht[a, d, j * B : (j + 1) * B, b * B : (b + 1) * B] = block.T.astype(BF16)

    def blk(ref, c, n=1):
        return ref.at[c * B : (c + n) * B]

    fs = (fsend, frecv)
    fc = {}
    for h in range(HALVES):
        for t in (1, 2, 3):
            t0, t1, t2, t3 = (tp.at[h, t, i] for i in range(4))
            plan = dict(
                r1=(blk(t1, 2), blk(t1, 0), right),
                l1=(blk(t1, 1), blk(t1, 3), left),
                r2=(blk(t2, 2), blk(t2, 0), right),
                l2=(blk(t2, 1), blk(t2, 3), left),
                dra=(blk(t1, 2), blk(t0, 0), diag_r),
                dla=(blk(t1, 1), blk(t0, 3), diag_l),
                drb=(blk(t1, 3), blk(t0, 1), diag_r),
                dlb=(blk(t1, 0), blk(t0, 2), diag_l),
                pa=(blk(t2, 1, 2), blk(t3, 1, 2), partner),
                p0=(blk(t2, 0), blk(t3, 0), partner),
                p3=(blk(t2, 3), blk(t3, 3), partner),
            )
            fc[t, h] = {
                name: Copy(src, dst, fs, (h, t - 1, n), who) for n, (name, (src, dst, who)) in enumerate(plan.items())
            }
    as_ = (asend, arecv)
    ac = {}
    for h in range(HALVES):
        for r in range(3):
            plan = dict(
                dl=(blk(s0.at[h, r], 0, 2), blk(rd.at[h, r], 2, 2), diag_l),
                dr=(blk(s0.at[h, r], 2, 2), blk(rd.at[h, r], 0, 2), diag_r),
                p=(s3.at[h, r], rp.at[h, r], partner),
                l1=(sc.at[h, r, 0, 0], rg.at[h, r, 0, 1], left),
                r1=(sc.at[h, r, 0, 1], rg.at[h, r, 0, 0], right),
                l2=(sc.at[h, r, 1, 0], rg.at[h, r, 1, 1], left),
                r2=(sc.at[h, r, 1, 1], rg.at[h, r, 1, 0], right),
            )
            ac[r, h] = {
                name: Copy(src, dst, as_, (h, r, n), who) for n, (name, (src, dst, who)) in enumerate(plan.items())
            }

    def cot_part(a, b, h):
        return cot_ref[real_row(a), b, :, h * width : (h + 1) * width].astype(F32)

    def adj_first(h):
        for a in range(2):
            for b in range(2):
                av[h, 4, a, b * B : (b + 1) * B] = (coef(4) * cot_part(a, b, h)).astype(BF16)

    def adj_partner(r, h):
        s3[h, r] = mm(ht[1, 2], av[h, 4 - r, 1]).astype(BF16)
        ac[r, h]["p"].start()

    def adj_diagonal(r, h):
        s0[h, r] = mm(ht[0, 0], av[h, 4 - r, 0]).astype(BF16)
        ac[r, h]["dl"].start()
        ac[r, h]["dr"].start()

    def adj_outer(r, h):
        adj_partner(r, h)
        adj_diagonal(r, h)

    def adj_inner(r, h):
        t = 4 - r
        qf[h, 1] = mm(ht[0, 2], av[h, t, 0]) + mm(ht[1, 1], av[h, t, 1])
        qf[h, 0] = mm(ht[0, 1], av[h, t, 0]) + mm(ht[1, 0], av[h, t, 1])

    def adj_side(r, h, a):
        c = ac[r, h]
        got, l, rt = (rd, "l1", "r1") if a == 0 else (rp, "l2", "r2")
        if a == 0:
            c["dl"].recv()
            c["dr"].recv()
        else:
            c["p"].recv()
        sc[h, r, a, 0] = (qf[h, a, 0:B] + got[h, r, 0:B].astype(F32)).astype(BF16)
        c[l].start()
        sc[h, r, a, 1] = (qf[h, a, 3 * B : 4 * B] + got[h, r, 3 * B : 4 * B].astype(F32)).astype(BF16)
        c[rt].start()

    def adj_finish(r, h, a):
        t = 3 - r
        c = ac[r, h]
        got, l, rt = (rd, "l1", "r1") if a == 0 else (rp, "l2", "r2")
        c[l].recv()
        c[rt].recv()
        for b in range(2):
            rows = slice((1 + b) * B, (2 + b) * B)
            own = slice(b * B, (b + 1) * B)
            total = qf[h, a, rows] + got[h, r, rows].astype(F32) + rg[h, r, a, b].astype(F32)
            scale = coef(t) - coef(4) if t == 2 else coef(t)
            value = scale * cot_part(a, b, h) + 2.0 * total
            if t == 1:
                value = value - af[h, a, own]
            if t == 3:
                af[h, a, own] = value
            av[h, t, a, own] = value.astype(BF16)

    def term_row(t, h, a):
        p = t - 1
        value = mm(hf[a, 0], tp[h, p, a]) + mm(hf[a, 1], tp[h, p, a + 1]) + mm(hf[a, 2], tp[h, p, a + 2])
        first = tp[h, 0, a + 1, B : 3 * B].astype(F32)
        if t == 1:
            acc[h, a] = coef(0) * first + coef(1) * value
        else:
            before = first if t == 2 else tf[h, t - 3, a]
            value = 2.0 * value - before
            total = acc[h, a] + coef(t) * value
            if t < 4:
                acc[h, a] = total
            else:
                for b in range(2):
                    den_ref[real_row(a), b, :, h * width : (h + 1) * width] = total[b * B : (b + 1) * B]
        if t < 3:
            tf[h, t - 1, a] = value
        if t < 4:
            tp[h, t, a + 1, B : 3 * B] = value.astype(BF16)
            c = fc[t, h]
            for name in ("r1", "l1", "dra", "dla") if a == 0 else ("pa", "r2", "l2"):
                c[name].start()

    def need(t, h, a):
        if t == 0:
            return
        c = fc[t, h]
        for name in ("r1", "l1", "r2", "l2") + (("dra", "dla", "drb", "dlb") if a == 0 else ("pa", "p0", "p3")):
            c[name].recv()

    def term(t, h):
        order = (0, 1) if t == 1 else (1, 0)
        for a in order:
            need(t - 1, h, a)
            term_row(t, h, a)

    def relay(t, h):
        c = fc[t, h]
        c["r2"].recv()
        c["p0"].start()
        c["l2"].recv()
        c["p3"].start()
        c["r1"].recv()
        c["dlb"].start()
        c["l1"].recv()
        c["drb"].start()

    def side(r, h):
        adj_side(r, h, 1)
        adj_side(r, h, 0)

    def finish(r, h):
        adj_finish(r, h, 1)
        adj_finish(r, h, 0)

    def gradient(t, first=False):
        for a in range(2):
            for d in range(3):
                full = mm_nt(joined(av, t, a), joined(tp, t - 1, a + d))
                for b in range(2):
                    for dy in range(3):
                        j = b + dy
                        piece = full[b * B : (b + 1) * B, j * B : (j + 1) * B]
                        if not first:
                            piece = piece + gacc[a, b, d * 3 + dy]
                        gacc[a, b, d * 3 + dy] = piece

    halves = range(HALVES)
    signs((0, 1, 2))
    in_cot.wait()
    for h in halves:
        adj_first(h)
    in_h[0].wait()
    select(0, 0)
    pl.semaphore_wait(barrier, 5)
    for h in halves:
        adj_diagonal(0, h)
    select(0, 1)
    select(0, 2)
    for h in halves:
        term_row(1, h, 0)
    signs((3,))
    in_h[1].wait()
    select(1, 2)
    for h in halves:
        adj_partner(0, h)
    select(1, 0)
    select(1, 1)
    for h in halves:
        term_row(1, h, 1)
    for h in halves:
        adj_inner(0, h)
    for t in (1, 2, 3):
        r = t - 1
        for h in halves:
            side(r, h)
            relay(t, h)
        if t < 3:
            for h in halves:
                finish(r, h)
                adj_outer(r + 1, h)
                term(t + 1, h)
                adj_inner(r + 1, h)
    gradient(2, first=True)
    gradient(3)
    for h in halves:
        term(4, h)
    gradient(4)
    for h in halves:
        finish(2, h)
    for group in list(fc.values()) + list(ac.values()):
        for one in group.values():
            one.sent()


def last_kernel(tp, av, gacc, den_ref, nbr_hbm, den_hbm, grad_hbm, grad_ref, sums, nbr_ref, osem):
    odd = lax.rem(lax.axis_index("gx"), 2)
    in_nbr = pltpu.make_async_copy(nbr_hbm, nbr_ref, osem.at[5])
    in_nbr.start()
    out_den = pltpu.make_async_copy(den_ref, den_hbm, osem.at[0])
    out_den.start()
    width = tp.shape[4]
    outs = []
    for a in range(2):
        ra = a + odd * (1 - 2 * a)
        for d in range(3):
            full = mm_nt(joined(av, 1, a), joined(tp, 0, a + d))
            for b in range(2):
                for dy in range(3):
                    j = b + dy
                    piece = full[b * B : (b + 1) * B, j * B : (j + 1) * B]
                    total = (piece + 2.0 * gacc[a, b, d * 3 + dy]) * (1.0 / (HALVES * width))
                    sums[a, b, d * 3 + dy] = total.astype(BF16)
        if a == 0:
            in_nbr.wait()
        for b in range(2):
            for k in range(8):
                code = nbr_ref[ra, b, k]
                rdx = code // 3
                mine = rdx + odd * (2 - 2 * rdx)
                grad_ref[a, b, k] = sums[a, b, mine * 3 + code - 3 * rdx]
            one = pltpu.make_async_copy(grad_ref.at[a, b], grad_hbm.at[ra, b], osem.at[1 + 2 * a + b])
            one.start()
            outs.append(one)
    out_den.wait()
    for one in outs:
        one.wait()


def shards(nx, ny, hamiltonian, neighbours, probe_seeds, coefficients, cotangent):
    width = cotangent.shape[3] // HALVES
    whole = pl.BlockSpec(memory_space=pltpu.VMEM)
    scalars = pl.BlockSpec(memory_space=pltpu.SMEM)
    far = pl.BlockSpec(memory_space=pltpu.HBM)
    vmem = pltpu.VMEM
    dma = pltpu.SemaphoreType.DMA
    inside = pl.BlockSpec(memory_space=pltpu.VMEM)
    kept = pl.pallas_call(
        functools.partial(kernel, nx, ny),
        out_shape=(
            vmem((HALVES, 4, 4, 4 * B, width), BF16),
            vmem((HALVES, 5, 2, 2 * B, width), BF16),
            vmem((2, 2, 9, B, B), F32),
            vmem(cotangent.shape, F32),
        ),
        in_specs=[far, scalars, whole, scalars, far],
        out_specs=(inside,) * 4,
        scratch_shapes=[
            vmem(hamiltonian.shape[1:], BF16),
            vmem(hamiltonian.shape[1:], BF16),
            vmem(cotangent.shape, BF16),
            vmem((2, 3, 2 * B, 4 * B), BF16),
            vmem((2, 3, 4 * B, 2 * B), BF16),
            vmem((HALVES, 2, 2, 2 * B, width), F32),
            vmem((HALVES, 2, 2 * B, width), F32),
            vmem((HALVES, 2, 2 * B, width), F32),
            vmem((HALVES, 2, 4 * B, width), F32),
            vmem((HALVES, 3, 4 * B, width), BF16),
            vmem((HALVES, 3, 4 * B, width), BF16),
            vmem((HALVES, 3, 4 * B, width), BF16),
            vmem((HALVES, 3, 4 * B, width), BF16),
            vmem((HALVES, 3, 2, 2, B, width), BF16),
            vmem((HALVES, 3, 2, 2, B, width), BF16),
            dma((HALVES, 3, 11)),
            dma((HALVES, 3, 11)),
            dma((HALVES, 3, 7)),
            dma((HALVES, 3, 7)),
            dma((3,)),
        ],
        compiler_params=pltpu.CompilerParams(
            collective_id=0, has_side_effects=True, vmem_limit_bytes=58654720
        ),
    )(hamiltonian, neighbours, probe_seeds.reshape(1, -1), coefficients, cotangent)
    return pl.pallas_call(
        last_kernel,
        out_shape=(
            jax.ShapeDtypeStruct(cotangent.shape, F32),
            jax.ShapeDtypeStruct(hamiltonian.shape, BF16),
        ),
        in_specs=[inside] * 4 + [far],
        out_specs=(far, far),
        scratch_shapes=[
            vmem(hamiltonian.shape, BF16), vmem((2, 2, 9, B, B), BF16),
            pltpu.SMEM(neighbours.shape, jnp.int32), dma((6,)),
        ],
        compiler_params=pltpu.CompilerParams(vmem_limit_bytes=16 * 1024 * 1024),
    )(*kept, neighbours)


def solution(mesh):
    placed = (
        P("gx", "gy", None, None, None),
        P("gx", "gy", None),
        P(),
        P(),
        P("gx", "gy", None, None),
    )
    return jax.shard_map(
        functools.partial(shards, mesh.shape["gx"], mesh.shape["gy"]),
        mesh=mesh,
        in_specs=placed,
        out_specs=(P("gx", "gy", None, None), P("gx", "gy", None, None, None)),
        check_vma=False,
    )
```

```python
import functools

import jax
import jax.numpy as jnp
from jax import lax
from jax.experimental import pallas as pl
from jax.experimental.pallas import tpu as pltpu
from jax.sharding import PartitionSpec as P

MESH = pl.DeviceIdType.MESH
BF16 = jnp.bfloat16
F32 = jnp.float32
B = 128
HALVES = 2
CUT = 4


def mm(left, right):
    return jnp.dot(left, right, preferred_element_type=F32)


def mm_nt(left, right):
    return lax.dot_general(left, right, (((1,), (1,)), ((), ())), preferred_element_type=F32)


def joined(ref, *where):
    return jnp.concatenate([ref[(h,) + where] for h in range(HALVES)], axis=1)


class Copy:
    def __init__(self, *args):
        self.args = args
        self.arrived = False

    def make(self):
        src, dst, sems, where, who = self.args
        return pltpu.make_async_remote_copy(
            src_ref=src, dst_ref=dst, send_sem=sems[0].at[where], recv_sem=sems[1].at[where],
            device_id=who, device_id_type=MESH,
        )

    def start(self):
        self.make().start()

    def recv(self):
        if not self.arrived:
            self.arrived = True
            self.make().wait_recv()

    def sent(self):
        self.make().wait_send()


def kernel(
    nx, ny,
    h_hbm, nbr_hbm, seed_hbm, coef_hbm, cot_hbm,
    tp, av, gacc, den_ref, codes,
    h_outer, h_inner, cot_ref, nbr_ref, seed_ref, coef_ref,
    hf, ht, tf, af, acc, qf,
    s0, s3, rd, rp, sc, rg,
    fsend, frecv, asend, arecv, isem,
):
    gx = lax.axis_index("gx")
    gy = lax.axis_index("gy")
    odd = lax.rem(gx, 2)
    out_x = lax.rem(gx + nx - 1 + 2 * odd, nx)
    par_x = gx + 1 - 2 * odd
    right_y = lax.rem(gy + 1, ny)
    left_y = lax.rem(gy + ny - 1, ny)
    partner = (par_x, gy)
    right = (gx, right_y)
    left = (gx, left_y)
    diag_r = (out_x, right_y)
    diag_l = (out_x, left_y)

    barrier = pltpu.get_barrier_semaphore()
    for who in (partner, right, left, diag_r, diag_l):
        pl.semaphore_signal(barrier, inc=1, device_id=who, device_id_type=MESH)
    def real_row(a):
        return a + odd * (1 - 2 * a)

    in_seed = pltpu.make_async_copy(seed_hbm, seed_ref, isem.at[0])
    in_nbr = pltpu.make_async_copy(nbr_hbm, nbr_ref, isem.at[1])
    in_coef = pltpu.make_async_copy(coef_hbm, coef_ref, isem.at[2])
    in_cot = pltpu.make_async_copy(cot_hbm, cot_ref, isem.at[3])
    in_h = [
        [
            pltpu.make_async_copy(h_hbm.at[real_row(a), b, k : k + CUT], ref.at[b, k : k + CUT], isem.at[4 + a])
            for b in range(2) for k in range(0, 8, CUT)
        ]
        for a, ref in enumerate((h_outer, h_inner))
    ]
    for one in [in_seed, in_nbr, in_coef] + in_h[0] + [in_cot] + in_h[1]:
        one.start()

    width = tp.shape[4]

    def coef(t):
        return coef_ref[t]

    def signs(rows):
        whole = HALVES * width
        lane_rows = lax.broadcasted_iota(jnp.int32, (B, whole), 0) * jnp.int32(-1640531535)
        seeds = jnp.broadcast_to(seed_ref[...], (B, whole))
        for i in rows:
            ri = i + odd * (3 - 2 * i)
            px = lax.rem(gx * 2 + ri - 1 + 2 * nx, 2 * nx)
            for j in range(4):
                py = lax.rem(gy * 2 + j - 1 + 2 * ny, 2 * ny)
                base = ((px * (2 * ny) + py) * B) * jnp.int32(-1640531535)
                hashed = (lane_rows + base) ^ seeds
                hashed = hashed ^ (hashed >> 15)
                hashed = hashed * jnp.int32(739982445)
                hashed = hashed ^ (hashed >> 12)
                sign = jnp.where((hashed & 128) == 0, 1.0, -1.0).astype(BF16)
                for h in range(HALVES):
                    tp[h, 0, i, j * B : (j + 1) * B] = sign[:, h * width : (h + 1) * width]

    def select(a, d):
        zero = jnp.zeros((B, B), BF16)
        ra = real_row(a)
        rdx = d + odd * (2 - 2 * d)
        hf[a, d, 0:B, 3 * B : 4 * B] = zero
        hf[a, d, B : 2 * B, 0:B] = zero
        ht[a, d, 3 * B : 4 * B, 0:B] = zero
        ht[a, d, 0:B, B : 2 * B] = zero
        for b in range(2):
            for dy in range(3):
                code = rdx * 3 + dy
                place = jnp.int32(0)
                for k in range(8):
                    place = jnp.where(nbr_ref[ra, b, k] == code, k + 1, place)
                found = jnp.where(place > 0, 1.0, 0.0)
                block = (h_outer, h_inner)[a][b, jnp.maximum(place - 1, 0)].astype(F32) * found
                j = b + dy
                hf[a, d, b * B : (b + 1) * B, j * B : (j + 1) * B] = block.astype(BF16)
                ht[a, d, j * B : (j + 1) * B, b * B : (b + 1) * B] = block.T.astype(BF16)

    def blk(ref, c, n=1):
        return ref.at[c * B : (c + n) * B]

    fs = (fsend, frecv)
    fc = {}
    for h in range(HALVES):
        for t in (1, 2, 3):
            t0, t1, t2, t3 = (tp.at[h, t, i] for i in range(4))
            plan = dict(
                r1=(blk(t1, 2), blk(t1, 0), right),
                l1=(blk(t1, 1), blk(t1, 3), left),
                r2=(blk(t2, 2), blk(t2, 0), right),
                l2=(blk(t2, 1), blk(t2, 3), left),
                dra=(blk(t1, 2), blk(t0, 0), diag_r),
                dla=(blk(t1, 1), blk(t0, 3), diag_l),
                drb=(blk(t1, 3), blk(t0, 1), diag_r),
                dlb=(blk(t1, 0), blk(t0, 2), diag_l),
                pa=(blk(t2, 1, 2), blk(t3, 1, 2), partner),
                p0=(blk(t2, 0), blk(t3, 0), partner),
                p3=(blk(t2, 3), blk(t3, 3), partner),
            )
            fc[t, h] = {
                name: Copy(src, dst, fs, (h, t - 1, n), who) for n, (name, (src, dst, who)) in enumerate(plan.items())
            }
    as_ = (asend, arecv)
    ac = {}
    for h in range(HALVES):
        for r in range(3):
            plan = dict(
                dl=(blk(s0.at[h, r], 0, 2), blk(rd.at[h, r], 2, 2), diag_l),
                dr=(blk(s0.at[h, r], 2, 2), blk(rd.at[h, r], 0, 2), diag_r),
                p=(s3.at[h, r], rp.at[h, r], partner),
                l1=(sc.at[h, r, 0, 0], rg.at[h, r, 0, 1], left),
                r1=(sc.at[h, r, 0, 1], rg.at[h, r, 0, 0], right),
                l2=(sc.at[h, r, 1, 0], rg.at[h, r, 1, 1], left),
                r2=(sc.at[h, r, 1, 1], rg.at[h, r, 1, 0], right),
            )
            ac[r, h] = {
                name: Copy(src, dst, as_, (h, r, n), who) for n, (name, (src, dst, who)) in enumerate(plan.items())
            }

    def cot_part(a, b, h):
        return cot_ref[real_row(a), b, :, h * width : (h + 1) * width].astype(F32)

    def adj_first(h):
        for a in range(2):
            for b in range(2):
                av[h, 4, a, b * B : (b + 1) * B] = (coef(4) * cot_part(a, b, h)).astype(BF16)

    def adj_partner(r, h):
        s3[h, r] = mm(ht[1, 2], av[h, 4 - r, 1]).astype(BF16)
        ac[r, h]["p"].start()

    def adj_diagonal(r, h):
        s0[h, r] = mm(ht[0, 0], av[h, 4 - r, 0]).astype(BF16)
        ac[r, h]["dl"].start()
        ac[r, h]["dr"].start()

    def adj_outer(r, h):
        adj_partner(r, h)
        adj_diagonal(r, h)

    def adj_inner(r, h):
        t = 4 - r
        qf[h, 1] = mm(ht[0, 2], av[h, t, 0]) + mm(ht[1, 1], av[h, t, 1])
        qf[h, 0] = mm(ht[0, 1], av[h, t, 0]) + mm(ht[1, 0], av[h, t, 1])

    def adj_side(r, h, a):
        c = ac[r, h]
        got, l, rt = (rd, "l1", "r1") if a == 0 else (rp, "l2", "r2")
        if a == 0:
            c["dl"].recv()
            c["dr"].recv()
        else:
            c["p"].recv()
        sc[h, r, a, 0] = (qf[h, a, 0:B] + got[h, r, 0:B].astype(F32)).astype(BF16)
        c[l].start()
        sc[h, r, a, 1] = (qf[h, a, 3 * B : 4 * B] + got[h, r, 3 * B : 4 * B].astype(F32)).astype(BF16)
        c[rt].start()

    def adj_finish(r, h, a):
        t = 3 - r
        c = ac[r, h]
        got, l, rt = (rd, "l1", "r1") if a == 0 else (rp, "l2", "r2")
        c[l].recv()
        c[rt].recv()
        for b in range(2):
            rows = slice((1 + b) * B, (2 + b) * B)
            own = slice(b * B, (b + 1) * B)
            total = qf[h, a, rows] + got[h, r, rows].astype(F32) + rg[h, r, a, b].astype(F32)
            scale = coef(t) - coef(4) if t == 2 else coef(t)
            value = scale * cot_part(a, b, h) + 2.0 * total
            if t == 1:
                value = value - af[h, a, own]
            if t == 3:
                af[h, a, own] = value
            av[h, t, a, own] = value.astype(BF16)

    def term_row(t, h, a):
        p = t - 1
        value = mm(hf[a, 0], tp[h, p, a]) + mm(hf[a, 1], tp[h, p, a + 1]) + mm(hf[a, 2], tp[h, p, a + 2])
        first = tp[h, 0, a + 1, B : 3 * B].astype(F32)
        if t == 1:
            acc[h, a] = coef(0) * first + coef(1) * value
        else:
            before = first if t == 2 else tf[h, t - 3, a]
            value = 2.0 * value - before
            total = acc[h, a] + coef(t) * value
            if t < 4:
                acc[h, a] = total
            else:
                for b in range(2):
                    den_ref[real_row(a), b, :, h * width : (h + 1) * width] = total[b * B : (b + 1) * B]
        if t < 3:
            tf[h, t - 1, a] = value
        if t < 4:
            tp[h, t, a + 1, B : 3 * B] = value.astype(BF16)
            c = fc[t, h]
            for name in ("r1", "l1", "dra", "dla") if a == 0 else ("pa", "r2", "l2"):
                c[name].start()

    def need(t, h, a):
        if t == 0:
            return
        c = fc[t, h]
        for name in ("r1", "l1", "r2", "l2") + (("dra", "dla", "drb", "dlb") if a == 0 else ("pa", "p0", "p3")):
            c[name].recv()

    def term(t, h):
        order = (0, 1) if t == 1 else (1, 0)
        for a in order:
            need(t - 1, h, a)
            term_row(t, h, a)

    def relay(t, h):
        c = fc[t, h]
        c["r2"].recv()
        c["p0"].start()
        c["l2"].recv()
        c["p3"].start()
        c["r1"].recv()
        c["dlb"].start()
        c["l1"].recv()
        c["drb"].start()

    def side(r, h):
        adj_side(r, h, 1)
        adj_side(r, h, 0)

    def finish(r, h):
        adj_finish(r, h, 1)
        adj_finish(r, h, 0)

    def gradient(t, first=False, outermost=(False, True)):
        for a in range(2):
            for d in range(3):
                if (a + d == 0) not in outermost:
                    continue
                full = mm_nt(joined(av, t, a), joined(tp, t - 1, a + d))
                for b in range(2):
                    for dy in range(3):
                        j = b + dy
                        piece = full[b * B : (b + 1) * B, j * B : (j + 1) * B]
                        if not first:
                            piece = piece + gacc[a, b, d * 3 + dy]
                        gacc[a, b, d * 3 + dy] = piece

    halves = range(HALVES)
    in_seed.wait()
    signs((0, 1, 2))
    in_nbr.wait()
    in_coef.wait()
    for n in range(32):
        codes[n : n + 1] = jnp.full((1, B), nbr_ref[n // 16, n // 8 % 2, n % 8], jnp.int32)
    in_cot.wait()
    for h in halves:
        adj_first(h)
    for one in in_h[0]:
        one.wait()
    select(0, 0)
    select(0, 1)
    select(0, 2)
    pl.semaphore_wait(barrier, 5)
    for h in halves:
        adj_diagonal(0, h)
        term_row(1, h, 0)
    signs((3,))
    for one in in_h[1]:
        one.wait()
    select(1, 2)
    for h in halves:
        adj_partner(0, h)
    select(1, 0)
    select(1, 1)
    for h in halves:
        term_row(1, h, 1)
    for h in halves:
        adj_inner(0, h)
    for t in (1, 2, 3):
        r = t - 1
        for h in halves:
            side(r, h)
            relay(t, h)
        if t < 3:
            for h in halves:
                finish(r, h)
                adj_outer(r + 1, h)
                term(t + 1, h)
            for h in halves:
                adj_inner(r + 1, h)
    gradient(2, first=True)
    gradient(3)
    for h in halves:
        need(3, h, 1)
        term_row(4, h, 1)
    gradient(4, outermost=(False,))
    for h in halves:
        finish(2, h)
    for h in halves:
        need(3, h, 0)
        term_row(4, h, 0)
    gradient(4, outermost=(True,))
    for group in list(fc.values()) + list(ac.values()):
        for one in group.values():
            one.sent()


def last_kernel(tp, av, gacc, den_ref, codes, den_hbm, grad_hbm, grad_ref, sums, nbr_ref, osem):
    odd = lax.rem(lax.axis_index("gx"), 2)
    in_nbr = pltpu.make_async_copy(codes, nbr_ref, osem.at[5])
    in_nbr.start()
    out_den = pltpu.make_async_copy(den_ref, den_hbm, osem.at[0])
    out_den.start()
    width = tp.shape[4]
    outs = []
    for a in range(2):
        ra = a + odd * (1 - 2 * a)
        for d in range(3):
            full = mm_nt(joined(av, 1, a), joined(tp, 0, a + d))
            for b in range(2):
                for dy in range(3):
                    j = b + dy
                    piece = full[b * B : (b + 1) * B, j * B : (j + 1) * B]
                    total = (piece + 2.0 * gacc[a, b, d * 3 + dy]) * (1.0 / (HALVES * width))
                    sums[a, b, d * 3 + dy] = total.astype(BF16)
        if a == 0:
            in_nbr.wait()
        for b in range(2):
            for k in range(8):
                code = nbr_ref[ra * 16 + b * 8 + k, 0]
                rdx = code // 3
                mine = rdx + odd * (2 - 2 * rdx)
                grad_ref[a, b, k] = sums[a, b, mine * 3 + code - 3 * rdx]
            one = pltpu.make_async_copy(grad_ref.at[a, b], grad_hbm.at[ra, b], osem.at[1 + 2 * a + b])
            one.start()
            outs.append(one)
    out_den.wait()
    for one in outs:
        one.wait()


def shards(nx, ny, hamiltonian, neighbours, probe_seeds, coefficients, cotangent):
    width = cotangent.shape[3] // HALVES
    far = pl.BlockSpec(memory_space=pltpu.HBM)
    vmem = pltpu.VMEM
    dma = pltpu.SemaphoreType.DMA
    inside = pl.BlockSpec(memory_space=pltpu.VMEM)
    kept = pl.pallas_call(
        functools.partial(kernel, nx, ny),
        out_shape=(
            vmem((HALVES, 4, 4, 4 * B, width), BF16),
            vmem((HALVES, 5, 2, 2 * B, width), BF16),
            vmem((2, 2, 9, B, B), F32),
            vmem(cotangent.shape, F32),
            vmem((32, B), jnp.int32),
        ),
        in_specs=[far] * 5,
        out_specs=(inside,) * 5,
        scratch_shapes=[
            vmem(hamiltonian.shape[1:], BF16),
            vmem(hamiltonian.shape[1:], BF16),
            vmem(cotangent.shape, BF16),
            pltpu.SMEM(neighbours.shape, jnp.int32),
            vmem((1, probe_seeds.shape[0]), jnp.int32),
            pltpu.SMEM(coefficients.shape, F32),
            vmem((2, 3, 2 * B, 4 * B), BF16),
            vmem((2, 3, 4 * B, 2 * B), BF16),
            vmem((HALVES, 2, 2, 2 * B, width), F32),
            vmem((HALVES, 2, 2 * B, width), F32),
            vmem((HALVES, 2, 2 * B, width), F32),
            vmem((HALVES, 2, 4 * B, width), F32),
            vmem((HALVES, 3, 4 * B, width), BF16),
            vmem((HALVES, 3, 4 * B, width), BF16),
            vmem((HALVES, 3, 4 * B, width), BF16),
            vmem((HALVES, 3, 4 * B, width), BF16),
            vmem((HALVES, 3, 2, 2, B, width), BF16),
            vmem((HALVES, 3, 2, 2, B, width), BF16),
            dma((HALVES, 3, 11)),
            dma((HALVES, 3, 11)),
            dma((HALVES, 3, 7)),
            dma((HALVES, 3, 7)),
            dma((6,)),
        ],
        compiler_params=pltpu.CompilerParams(
            collective_id=0, has_side_effects=True, vmem_limit_bytes=58638336
        ),
    )(hamiltonian, neighbours, probe_seeds.reshape(1, -1), coefficients, cotangent)
    return pl.pallas_call(
        last_kernel,
        out_shape=(
            jax.ShapeDtypeStruct(cotangent.shape, F32),
            jax.ShapeDtypeStruct(hamiltonian.shape, BF16),
        ),
        in_specs=[inside] * 5,
        out_specs=(far, far),
        scratch_shapes=[
            vmem(hamiltonian.shape, BF16), vmem((2, 2, 9, B, B), BF16),
            pltpu.SMEM((32, B), jnp.int32), dma((6,)),
        ],
        compiler_params=pltpu.CompilerParams(vmem_limit_bytes=16 * 1024 * 1024),
    )(*kept)


def solution(mesh):
    placed = (
        P("gx", "gy", None, None, None),
        P("gx", "gy", None),
        P(),
        P(),
        P("gx", "gy", None, None),
    )
    return jax.shard_map(
        functools.partial(shards, mesh.shape["gx"], mesh.shape["gy"]),
        mesh=mesh,
        in_specs=placed,
        out_specs=(P("gx", "gy", None, None), P("gx", "gy", None, None, None)),
        check_vma=False,
    )
```

```python
import functools

import jax
import jax.numpy as jnp
from jax import lax
from jax.experimental import pallas as pl
from jax.experimental.pallas import tpu as pltpu
from jax.sharding import PartitionSpec as P

MESH = pl.DeviceIdType.MESH
BF16 = jnp.bfloat16
F32 = jnp.float32
B = 128
HALVES = 2
CUT = 4


def mm(left, right):
    return jnp.dot(left, right, preferred_element_type=F32)


def mm_nt(left, right):
    return lax.dot_general(left, right, (((1,), (1,)), ((), ())), preferred_element_type=F32)


def joined(ref, *where):
    return jnp.concatenate([ref[(h,) + where] for h in range(HALVES)], axis=1)


class Copy:
    def __init__(self, *args):
        self.args = args
        self.arrived = False

    def make(self):
        src, dst, sems, where, who = self.args
        return pltpu.make_async_remote_copy(
            src_ref=src, dst_ref=dst, send_sem=sems[0].at[where], recv_sem=sems[1].at[where],
            device_id=who, device_id_type=MESH,
        )

    def start(self):
        self.make().start()

    def recv(self):
        if not self.arrived:
            self.arrived = True
            self.make().wait_recv()

    def sent(self):
        self.make().wait_send()


def kernel(
    nx, ny,
    h_hbm, nbr_hbm, seed_hbm, coef_hbm, cot_hbm,
    tp, av, gacc, den_ref, codes,
    h_outer, h_inner, cot_ref, nbr_ref, seed_ref, coef_ref,
    hf, ht, tf, af, acc, qf,
    s0, s3, rd, rp, sc, rg,
    fsend, frecv, asend, arecv, isem,
):
    gx = lax.axis_index("gx")
    gy = lax.axis_index("gy")
    odd = lax.rem(gx, 2)
    out_x = lax.rem(gx + nx - 1 + 2 * odd, nx)
    par_x = gx + 1 - 2 * odd
    right_y = lax.rem(gy + 1, ny)
    left_y = lax.rem(gy + ny - 1, ny)
    partner = (par_x, gy)
    right = (gx, right_y)
    left = (gx, left_y)
    diag_r = (out_x, right_y)
    diag_l = (out_x, left_y)

    barrier = pltpu.get_barrier_semaphore()
    for who in (partner, right, left, diag_r, diag_l):
        pl.semaphore_signal(barrier, inc=1, device_id=who, device_id_type=MESH)
    def real_row(a):
        return a + odd * (1 - 2 * a)

    in_seed = pltpu.make_async_copy(seed_hbm, seed_ref, isem.at[0])
    in_nbr = pltpu.make_async_copy(nbr_hbm, nbr_ref, isem.at[1])
    in_coef = pltpu.make_async_copy(coef_hbm, coef_ref, isem.at[2])
    in_cot = pltpu.make_async_copy(cot_hbm, cot_ref, isem.at[3])
    in_h = [
        [
            pltpu.make_async_copy(h_hbm.at[real_row(a), b, k : k + CUT], ref.at[b, k : k + CUT], isem.at[4 + a])
            for b in range(2) for k in range(0, 8, CUT)
        ]
        for a, ref in enumerate((h_outer, h_inner))
    ]
    for one in [in_seed, in_nbr, in_coef] + in_h[0] + [in_cot] + in_h[1]:
        one.start()

    width = tp.shape[4]

    def coef(t):
        return coef_ref[t]

    def signs(rows):
        whole = HALVES * width
        lane_rows = lax.broadcasted_iota(jnp.int32, (B, whole), 0) * jnp.int32(-1640531535)
        seeds = jnp.broadcast_to(seed_ref[...], (B, whole))
        for i in rows:
            ri = i + odd * (3 - 2 * i)
            px = lax.rem(gx * 2 + ri - 1 + 2 * nx, 2 * nx)
            for j in range(4):
                py = lax.rem(gy * 2 + j - 1 + 2 * ny, 2 * ny)
                base = ((px * (2 * ny) + py) * B) * jnp.int32(-1640531535)
                hashed = (lane_rows + base) ^ seeds
                hashed = hashed ^ (hashed >> 15)
                hashed = hashed * jnp.int32(739982445)
                hashed = hashed ^ (hashed >> 12)
                sign = jnp.where((hashed & 128) == 0, 1.0, -1.0).astype(BF16)
                for h in range(HALVES):
                    tp[h, 0, i, j * B : (j + 1) * B] = sign[:, h * width : (h + 1) * width]

    def select(a, d):
        zero = jnp.zeros((B, B), BF16)
        ra = real_row(a)
        rdx = d + odd * (2 - 2 * d)
        hf[a, d, 0:B, 3 * B : 4 * B] = zero
        hf[a, d, B : 2 * B, 0:B] = zero
        ht[a, d, 3 * B : 4 * B, 0:B] = zero
        ht[a, d, 0:B, B : 2 * B] = zero
        for b in range(2):
            for dy in range(3):
                code = rdx * 3 + dy
                place = jnp.int32(0)
                for k in range(8):
                    place = jnp.where(nbr_ref[ra, b, k] == code, k + 1, place)
                found = jnp.where(place > 0, 1.0, 0.0)
                block = (h_outer, h_inner)[a][b, jnp.maximum(place - 1, 0)].astype(F32) * found
                j = b + dy
                hf[a, d, b * B : (b + 1) * B, j * B : (j + 1) * B] = block.astype(BF16)
                ht[a, d, j * B : (j + 1) * B, b * B : (b + 1) * B] = block.T.astype(BF16)

    def blk(ref, c, n=1):
        return ref.at[c * B : (c + n) * B]

    fs = (fsend, frecv)
    fc = {}
    for h in range(HALVES):
        for t in (1, 2, 3):
            t0, t1, t2, t3 = (tp.at[h, t, i] for i in range(4))
            plan = dict(
                r1=(blk(t1, 2), blk(t1, 0), right),
                l1=(blk(t1, 1), blk(t1, 3), left),
                r2=(blk(t2, 2), blk(t2, 0), right),
                l2=(blk(t2, 1), blk(t2, 3), left),
                dra=(blk(t1, 2), blk(t0, 0), diag_r),
                dla=(blk(t1, 1), blk(t0, 3), diag_l),
                drb=(blk(t1, 3), blk(t0, 1), diag_r),
                dlb=(blk(t1, 0), blk(t0, 2), diag_l),
                pa=(blk(t2, 1, 2), blk(t3, 1, 2), partner),
                p0=(blk(t2, 0), blk(t3, 0), partner),
                p3=(blk(t2, 3), blk(t3, 3), partner),
            )
            fc[t, h] = {
                name: Copy(src, dst, fs, (h, t - 1, n), who) for n, (name, (src, dst, who)) in enumerate(plan.items())
            }
    as_ = (asend, arecv)
    ac = {}
    for h in range(HALVES):
        for r in range(3):
            plan = dict(
                dl=(blk(s0.at[h, r], 0, 2), blk(rd.at[h, r], 2, 2), diag_l),
                dr=(blk(s0.at[h, r], 2, 2), blk(rd.at[h, r], 0, 2), diag_r),
                p=(s3.at[h, r], rp.at[h, r], partner),
                l1=(sc.at[h, r, 0, 0], rg.at[h, r, 0, 1], left),
                r1=(sc.at[h, r, 0, 1], rg.at[h, r, 0, 0], right),
                l2=(sc.at[h, r, 1, 0], rg.at[h, r, 1, 1], left),
                r2=(sc.at[h, r, 1, 1], rg.at[h, r, 1, 0], right),
            )
            ac[r, h] = {
                name: Copy(src, dst, as_, (h, r, n), who) for n, (name, (src, dst, who)) in enumerate(plan.items())
            }

    def cot_part(a, b, h):
        return cot_ref[real_row(a), b, :, h * width : (h + 1) * width].astype(F32)

    def adj_first(h):
        for a in range(2):
            for b in range(2):
                av[h, 4, a, b * B : (b + 1) * B] = (coef(4) * cot_part(a, b, h)).astype(BF16)

    def adj_partner(r, h):
        s3[h, r] = mm(ht[1, 2], av[h, 4 - r, 1]).astype(BF16)
        ac[r, h]["p"].start()

    def adj_diagonal(r, h):
        s0[h, r] = mm(ht[0, 0], av[h, 4 - r, 0]).astype(BF16)
        ac[r, h]["dl"].start()
        ac[r, h]["dr"].start()

    def adj_outer(r, h):
        adj_partner(r, h)
        adj_diagonal(r, h)

    def adj_inner(r, h):
        t = 4 - r
        qf[h, 1] = mm(ht[0, 2], av[h, t, 0]) + mm(ht[1, 1], av[h, t, 1])
        qf[h, 0] = mm(ht[0, 1], av[h, t, 0]) + mm(ht[1, 0], av[h, t, 1])

    def adj_side(r, h, a):
        c = ac[r, h]
        got, l, rt = (rd, "l1", "r1") if a == 0 else (rp, "l2", "r2")
        if a == 0:
            c["dl"].recv()
            c["dr"].recv()
        else:
            c["p"].recv()
        sc[h, r, a, 0] = (qf[h, a, 0:B] + got[h, r, 0:B].astype(F32)).astype(BF16)
        c[l].start()
        sc[h, r, a, 1] = (qf[h, a, 3 * B : 4 * B] + got[h, r, 3 * B : 4 * B].astype(F32)).astype(BF16)
        c[rt].start()

    def adj_finish(r, h, a):
        t = 3 - r
        c = ac[r, h]
        got, l, rt = (rd, "l1", "r1") if a == 0 else (rp, "l2", "r2")
        c[l].recv()
        c[rt].recv()
        for b in range(2):
            rows = slice((1 + b) * B, (2 + b) * B)
            own = slice(b * B, (b + 1) * B)
            total = qf[h, a, rows] + got[h, r, rows].astype(F32) + rg[h, r, a, b].astype(F32)
            scale = coef(t) - coef(4) if t == 2 else coef(t)
            value = scale * cot_part(a, b, h) + 2.0 * total
            if t == 1:
                value = value - af[h, a, own]
            if t == 3:
                af[h, a, own] = value
            av[h, t, a, own] = value.astype(BF16)

    def term_row(t, h, a):
        p = t - 1
        value = mm(hf[a, 0], tp[h, p, a]) + mm(hf[a, 1], tp[h, p, a + 1]) + mm(hf[a, 2], tp[h, p, a + 2])
        first = tp[h, 0, a + 1, B : 3 * B].astype(F32)
        if t == 1:
            acc[h, a] = coef(0) * first + coef(1) * value
        else:
            before = first if t == 2 else tf[h, t - 3, a]
            value = 2.0 * value - before
            total = acc[h, a] + coef(t) * value
            if t < 4:
                acc[h, a] = total
            else:
                for b in range(2):
                    den_ref[real_row(a), b, :, h * width : (h + 1) * width] = total[b * B : (b + 1) * B]
        if t < 3:
            tf[h, t - 1, a] = value
        if t < 4:
            tp[h, t, a + 1, B : 3 * B] = value.astype(BF16)
            c = fc[t, h]
            for name in ("r1", "l1", "dra", "dla") if a == 0 else ("pa", "r2", "l2"):
                c[name].start()

    def need(t, h, a):
        if t == 0:
            return
        c = fc[t, h]
        for name in ("r1", "l1", "r2", "l2") + (("dra", "dla", "drb", "dlb") if a == 0 else ("pa", "p0", "p3")):
            c[name].recv()

    def term(t, h):
        order = (0, 1) if t == 1 else (1, 0)
        for a in order:
            need(t - 1, h, a)
            term_row(t, h, a)

    def relay(t, h):
        c = fc[t, h]
        c["r2"].recv()
        c["p0"].start()
        c["l2"].recv()
        c["p3"].start()
        c["r1"].recv()
        c["dlb"].start()
        c["l1"].recv()
        c["drb"].start()

    def side(r, h):
        adj_side(r, h, 1)
        adj_side(r, h, 0)

    def finish(r, h):
        adj_finish(r, h, 1)
        adj_finish(r, h, 0)

    def gradient(t, first=False, outermost=(False, True)):
        for a in range(2):
            for d in range(3):
                if (a + d == 0) not in outermost:
                    continue
                full = mm_nt(joined(av, t, a), joined(tp, t - 1, a + d))
                for b in range(2):
                    for dy in range(3):
                        j = b + dy
                        piece = full[b * B : (b + 1) * B, j * B : (j + 1) * B]
                        if not first:
                            piece = piece + gacc[a, b, d * 3 + dy]
                        gacc[a, b, d * 3 + dy] = piece

    halves = range(HALVES)
    in_seed.wait()
    signs((0, 1, 2))
    in_nbr.wait()
    in_coef.wait()
    for n in range(32):
        codes[n : n + 1] = jnp.full((1, B), nbr_ref[n // 16, n // 8 % 2, n % 8], jnp.int32)
    in_cot.wait()
    for h in halves:
        adj_first(h)
    for one in in_h[0]:
        one.wait()
    select(0, 0)
    select(0, 1)
    select(0, 2)
    pl.semaphore_wait(barrier, 5)
    for h in halves:
        adj_diagonal(0, h)
        term_row(1, h, 0)
    signs((3,))
    for one in in_h[1]:
        one.wait()
    select(1, 2)
    for h in halves:
        adj_partner(0, h)
    select(1, 0)
    select(1, 1)
    for h in halves:
        term_row(1, h, 1)
    for h in halves:
        adj_inner(0, h)
    for t in (1, 2, 3):
        r = t - 1
        for h in halves:
            side(r, h)
            relay(t, h)
        if t < 3:
            for h in halves:
                adj_finish(r, h, 1)
                adj_partner(r + 1, h)
                adj_finish(r, h, 0)
                adj_diagonal(r + 1, h)
                term(t + 1, h)
            for h in halves:
                adj_inner(r + 1, h)
    gradient(2, first=True)
    gradient(3)
    for h in halves:
        need(3, h, 1)
        term_row(4, h, 1)
    gradient(4, outermost=(False,))
    for h in halves:
        finish(2, h)
    for h in halves:
        need(3, h, 0)
        term_row(4, h, 0)
    gradient(4, outermost=(True,))
    for group in list(fc.values()) + list(ac.values()):
        for one in group.values():
            one.sent()


def last_kernel(tp, av, gacc, den_ref, codes, den_hbm, grad_hbm, grad_ref, sums, nbr_ref, osem):
    odd = lax.rem(lax.axis_index("gx"), 2)
    in_nbr = pltpu.make_async_copy(codes, nbr_ref, osem.at[5])
    in_nbr.start()
    out_den = pltpu.make_async_copy(den_ref, den_hbm, osem.at[0])
    out_den.start()
    width = tp.shape[4]
    outs = []
    for a in range(2):
        ra = a + odd * (1 - 2 * a)
        for d in range(3):
            full = mm_nt(joined(av, 1, a), joined(tp, 0, a + d))
            for b in range(2):
                for dy in range(3):
                    j = b + dy
                    piece = full[b * B : (b + 1) * B, j * B : (j + 1) * B]
                    total = (piece + 2.0 * gacc[a, b, d * 3 + dy]) * (1.0 / (HALVES * width))
                    sums[a, b, d * 3 + dy] = total.astype(BF16)
        if a == 0:
            in_nbr.wait()
        for b in range(2):
            for k in range(8):
                code = nbr_ref[ra * 16 + b * 8 + k, 0]
                rdx = code // 3
                mine = rdx + odd * (2 - 2 * rdx)
                grad_ref[a, b, k] = sums[a, b, mine * 3 + code - 3 * rdx]
            one = pltpu.make_async_copy(grad_ref.at[a, b], grad_hbm.at[ra, b], osem.at[1 + 2 * a + b])
            one.start()
            outs.append(one)
    out_den.wait()
    for one in outs:
        one.wait()


def shards(nx, ny, hamiltonian, neighbours, probe_seeds, coefficients, cotangent):
    width = cotangent.shape[3] // HALVES
    far = pl.BlockSpec(memory_space=pltpu.HBM)
    vmem = pltpu.VMEM
    dma = pltpu.SemaphoreType.DMA
    inside = pl.BlockSpec(memory_space=pltpu.VMEM)
    kept = pl.pallas_call(
        functools.partial(kernel, nx, ny),
        out_shape=(
            vmem((HALVES, 4, 4, 4 * B, width), BF16),
            vmem((HALVES, 5, 2, 2 * B, width), BF16),
            vmem((2, 2, 9, B, B), F32),
            vmem(cotangent.shape, F32),
            vmem((32, B), jnp.int32),
        ),
        in_specs=[far] * 5,
        out_specs=(inside,) * 5,
        scratch_shapes=[
            vmem(hamiltonian.shape[1:], BF16),
            vmem(hamiltonian.shape[1:], BF16),
            vmem(cotangent.shape, BF16),
            pltpu.SMEM(neighbours.shape, jnp.int32),
            vmem((1, probe_seeds.shape[0]), jnp.int32),
            pltpu.SMEM(coefficients.shape, F32),
            vmem((2, 3, 2 * B, 4 * B), BF16),
            vmem((2, 3, 4 * B, 2 * B), BF16),
            vmem((HALVES, 2, 2, 2 * B, width), F32),
            vmem((HALVES, 2, 2 * B, width), F32),
            vmem((HALVES, 2, 2 * B, width), F32),
            vmem((HALVES, 2, 4 * B, width), F32),
            vmem((HALVES, 3, 4 * B, width), BF16),
            vmem((HALVES, 3, 4 * B, width), BF16),
            vmem((HALVES, 3, 4 * B, width), BF16),
            vmem((HALVES, 3, 4 * B, width), BF16),
            vmem((HALVES, 3, 2, 2, B, width), BF16),
            vmem((HALVES, 3, 2, 2, B, width), BF16),
            dma((HALVES, 3, 11)),
            dma((HALVES, 3, 11)),
            dma((HALVES, 3, 7)),
            dma((HALVES, 3, 7)),
            dma((6,)),
        ],
        compiler_params=pltpu.CompilerParams(
            collective_id=0, has_side_effects=True, vmem_limit_bytes=58638336
        ),
    )(hamiltonian, neighbours, probe_seeds.reshape(1, -1), coefficients, cotangent)
    return pl.pallas_call(
        last_kernel,
        out_shape=(
            jax.ShapeDtypeStruct(cotangent.shape, F32),
            jax.ShapeDtypeStruct(hamiltonian.shape, BF16),
        ),
        in_specs=[inside] * 5,
        out_specs=(far, far),
        scratch_shapes=[
            vmem(hamiltonian.shape, BF16), vmem((2, 2, 9, B, B), BF16),
            pltpu.SMEM((32, B), jnp.int32), dma((6,)),
        ],
        compiler_params=pltpu.CompilerParams(vmem_limit_bytes=16 * 1024 * 1024),
    )(*kept)


def solution(mesh):
    placed = (
        P("gx", "gy", None, None, None),
        P("gx", "gy", None),
        P(),
        P(),
        P("gx", "gy", None, None),
    )
    return jax.shard_map(
        functools.partial(shards, mesh.shape["gx"], mesh.shape["gy"]),
        mesh=mesh,
        in_specs=placed,
        out_specs=(P("gx", "gy", None, None), P("gx", "gy", None, None, None)),
        check_vma=False,
    )
```
